256 devices in a mesh: row: 8 (over y, z_lo), col: 32 (over x, z_hi, core).
Axes of the slice: x: 4, y: 4, z: 8 (z_hi: 4, z_lo: 2; z = z_hi * 2 + z_lo), core: 2. Of those that a mesh axis runs over, the one named last changes fastest.
Arguments:
- x_init: float32 [4096, 64, 128], P(('row', 'col')), may hold values from -6 to 6
- gen_blocks: bfloat16 [8, 32, 256, 128, 128], P('row', 'col'), may hold values from -0.09375 to 0.09375
- blk_src: int32 [8, 32, 256], P('row', 'col'), may hold values from 0 to 511, as said below
- blk_dst: int32 [8, 32, 256], P('row', 'col'), may hold values from 0 to 127
- reward: int32 [4096, 128], P(('row', 'col')), may hold values 0 or 1
- horizon: float32 [1], replicated, may hold values from 1.5 to 4
Outputs:
- state: float32 [4096, 64, 128], P(('row', 'col'))
- accumulated: float32 [4096, 64, 128], P(('row', 'col'))
The draws below stay inside these ranges and needn't reach their ends.
Inputs may be any that keep to these rules, and one draw needn't show every extreme that they name: `blk_src`: on each device, slot j names a block-row in [(j // 8) * 16, (j // 8 + 1) * 16), and the 8 slots of one such group name distinct block-rows.
All inputs are finite; a program needn't handle non-finite values. No bound on the sum of `reward` on one device may be relied on, other than what follows from the above.
Results may differ from the reference program's by a relative error of at most 0.0021.
Values may be sent and summed in bfloat16 or wider, within the bound.
No kernel may reach another device: no remote copies, remote signals or barrier semaphores. Data moves between devices by JAX's collectives and lax.ppermute only.
A program may use at most 64 MiB of HBM per device.

```python
import jax
import jax.numpy as jnp
from jax import lax

BS = 128
NNZ = 16
STEPS = 3
CONFIGS = 64
SPAN_BLK = 16
STATES = 524288
SRC_BLK = 512
DST_BLK = 128
NB_DEV = 256
N_ROW = 8
N_COL = 32


def draw_blk_src(key, part):
    groups = N_ROW * N_COL * N_COL
    per_peer = SPAN_BLK * NNZ // N_COL
    subkeys = jax.random.split(key, groups)
    shuffled = jax.vmap(lambda sub: jax.random.permutation(sub, SPAN_BLK))(subkeys).astype(jnp.int32)
    steps = jnp.arange(per_peer, dtype=jnp.int32)[None, :]
    drawn = shuffled[:, :per_peer]
    low_pos = jnp.argmax(shuffled == 0, axis=1).astype(jnp.int32)
    high_pos = jnp.argmax(shuffled == SPAN_BLK - 1, axis=1).astype(jnp.int32)
    with_low = jnp.take_along_axis(shuffled, (low_pos[:, None] + steps) % SPAN_BLK, axis=1)
    with_high = jnp.take_along_axis(shuffled, (high_pos[:, None] + steps) % SPAN_BLK, axis=1)
    order_key = jax.random.fold_in(key, 7)
    order_keys = jax.random.split(order_key, groups)
    order = jax.vmap(lambda sub: jax.random.permutation(sub, per_peer))(order_keys).astype(jnp.int32)
    with_low = jnp.take_along_axis(with_low, order, axis=1)
    with_high = jnp.take_along_axis(with_high, order, axis=1)
    group_ids = jnp.arange(groups, dtype=jnp.int32)[:, None]
    chosen = jnp.where(group_ids == 0, with_low, drawn)
    chosen = jnp.where(group_ids == N_COL - 1, with_high, chosen)
    chosen = chosen.reshape(N_ROW, N_COL, N_COL, per_peer)
    chosen = chosen + (jnp.arange(N_COL, dtype=jnp.int32) * SPAN_BLK)[None, None, :, None]
    return chosen.reshape(N_ROW, N_COL, N_COL * per_peer).astype(jnp.int32)


def place_ends(array, rng, low, high):
    longest = array.shape.index(max(array.shape))
    spots = []
    for shift in (0, 1):
        where = [jax.random.randint(jax.random.fold_in(rng, axis), (), 0, length) for axis, length in enumerate(array.shape)]
        where[longest] = (where[longest] + shift) % array.shape[longest]
        spots.append(tuple(where))
    return array.at[spots[0]].set(low).at[spots[1]].set(high)


def shard_levels(rng, dims, pieces, smallest, high):
    level = 1.0
    for axis_at, blocks in pieces:
        steps = jax.random.uniform(jax.random.fold_in(jax.random.fold_in(rng, 6), axis_at), (blocks,), jnp.float32, smallest / len(pieces), high / len(pieces))
        level = level * jnp.repeat(jnp.exp(steps), dims[axis_at] // blocks).reshape((-1,) + (1,) * (len(dims) - 1 - axis_at))
    return level


def normal_values(key, extent, scale, reach, cuts=(), kind=jnp.bfloat16):
    loudness = shard_levels(key, extent, cuts, -0.22, 0.18) if cuts else 1.0
    array = jax.random.normal(key, extent, jnp.float32) * scale * loudness
    return jnp.minimum(jnp.maximum(array, -reach), reach).astype(kind)


def setup_inputs(seed: int = 0) -> dict:
    key_of = jax.random.split(jax.random.key(seed), 7)
    return {
        "x_init": normal_values(key_of[0], (STATES // BS, CONFIGS, BS), 1.0, 6.0, ((0, 256),), jnp.float32),
        "gen_blocks": normal_values(key_of[1], (N_ROW, N_COL, NB_DEV, BS, BS), (2 * NNZ * BS) ** -0.5, 0.09375, ((0, 8), (1, 32))),
        "blk_src": draw_blk_src(jax.random.fold_in(key_of[6], 71), 0),
        "blk_dst": place_ends(jax.random.randint(key_of[3], (N_ROW, N_COL, NB_DEV), 0, DST_BLK), jax.random.fold_in(key_of[3], 1), 0, DST_BLK - 1).astype(jnp.int32),
        "reward": place_ends((jax.random.randint(key_of[4], (STATES // BS, BS), 0, 2) < 1).astype(jnp.int32), jax.random.fold_in(key_of[4], 1), 0, 1),
        "horizon": jnp.clip(jax.random.uniform(key_of[5], (1,), jnp.float32, 1.5, 4.0), 1.5, 4.0),
    }


def poisson_weights(horizon):
    rate_time = horizon[0]
    poisson_term = jnp.exp(-rate_time)
    cumulated = poisson_term
    weights = [(1.0 - cumulated) / rate_time]
    for iteration in range(STEPS):
        poisson_term = poisson_term * rate_time / (iteration + 1.0)
        cumulated = cumulated + poisson_term
        weights.append((1.0 - cumulated) / rate_time)
    return weights


def reference(x_init, gen_blocks, blk_src, blk_dst, reward, horizon):
    row_ids = jnp.arange(N_ROW, dtype=jnp.int32)[:, None, None]
    col_ids = jnp.arange(N_COL, dtype=jnp.int32)[None, :, None]
    source_ids = (row_ids * SRC_BLK + blk_src).reshape(N_ROW * N_COL, NB_DEV).astype(jnp.int32)
    target_ids = (((blk_dst // SPAN_BLK) * N_COL + col_ids) * SPAN_BLK + blk_dst % SPAN_BLK)
    target_ids = target_ids.reshape(N_ROW * N_COL, NB_DEV).astype(jnp.int32)
    blocks = gen_blocks.reshape(N_ROW * N_COL, NB_DEV, BS, BS)
    weights = poisson_weights(horizon)
    reward_f = reward.astype(jnp.float32)[:, None, :]
    state = x_init
    accumulated = weights[0] * reward_f * state
    for iteration in range(STEPS):
        rounded = state.astype(jnp.bfloat16)

        def add_device(running, member):
            src_row, dst_col, tiles = member
            products = jnp.einsum("ncb,nbk->nck", rounded[src_row].astype(jnp.float32), tiles.astype(jnp.float32))
            return running.at[dst_col].add(products), None

        total, unused = lax.scan(add_device, jnp.zeros(state.shape, jnp.float32), (source_ids, target_ids, blocks))
        state = state + total
        accumulated = accumulated + weights[iteration + 1] * reward_f * state
    return state, accumulated
```

```python
import jax
import jax.numpy as jnp
from jax import lax
from jax.experimental import pallas as pl
from jax.experimental.pallas import tpu as pltpu
from jax.sharding import Mesh, PartitionSpec as P

STEPS = 3
AXES = ("y", "zl", "x", "zh", "core")
SHAPE = (4, 2, 4, 4, 2)
ROW = ("y", "zl")
COL = ("x", "zh", "core")
GROUPS = 8


def poisson_weights(horizon):
    rate_time = horizon[0]
    poisson_term = jnp.exp(-rate_time)
    cumulated = poisson_term
    weights = [(1.0 - cumulated) / rate_time]
    for iteration in range(STEPS):
        poisson_term = poisson_term * rate_time / (iteration + 1.0)
        cumulated = cumulated + poisson_term
        weights.append((1.0 - cumulated) / rate_time)
    return weights


def product_body(src, dst, order, x_ref, blk_ref, own_ref, *rest):
    sends, acc = rest[:-1], rest[-1]
    step = pl.program_id(0)
    slots = blk_ref.shape[0]
    held = x_ref.shape[0]
    span = own_ref.shape[0]

    @pl.when(step == 0)
    def _():
        acc[...] = jnp.zeros_like(acc)

    for slot in range(slots):
        at = step * slots + slot
        vectors = x_ref[src[at] - step * held]
        into = dst[at]
        acc[into] += jnp.dot(vectors, blk_ref[slot], preferred_element_type=jnp.float32)

    @pl.when(step == pl.num_programs(0) - 1)
    def _():
        own_ref[...] = acc[pl.ds(order[0] * span, span)]
        for place, send in enumerate(sends):
            send[...] = acc[pl.ds(order[place + 1] * span, span)].astype(send.dtype)


def products(src, dst, order, whole, blocks, rows, span):
    n, block_len, _ = blocks.shape
    configs = whole.shape[1]
    piece = (span, configs, block_len)
    outs = [jax.ShapeDtypeStruct(piece, jnp.float32)]
    outs += [jax.ShapeDtypeStruct(piece, jnp.bfloat16)] * (rows - 1)
    return pl.pallas_call(
        product_body,
        out_shape=outs,
        grid_spec=pltpu.PrefetchScalarGridSpec(
            num_scalar_prefetch=3,
            grid=(GROUPS,),
            in_specs=[
                pl.BlockSpec((whole.shape[0] // GROUPS, configs, block_len), lambda i, *_: (i, 0, 0)),
                pl.BlockSpec((n // GROUPS, block_len, block_len), lambda i, *_: (i, 0, 0)),
            ],
            out_specs=[pl.BlockSpec(piece, lambda i, *_: (0, 0, 0))] * rows,
            scratch_shapes=[pltpu.VMEM((rows * span, configs, block_len), jnp.float32)],
        ),
        compiler_params=pltpu.CompilerParams(vmem_limit_bytes=40 << 20),
        cost_estimate=pl.CostEstimate(
            flops=2 * n * configs * block_len * block_len,
            bytes_accessed=2 * (whole.size + blocks.size + rows * span * configs * block_len),
            transcendentals=0,
        ),
        name="products",
    )(src, dst, order, whole, blocks)


def shifted(dy, dzl):
    ny, nzl = SHAPE[0], SHAPE[1]
    return [
        (y * nzl + zl, (y + dy) % ny * nzl + (zl + dzl) % nzl)
        for y in range(ny)
        for zl in range(nzl)
    ]


def shards(x_init, gen_blocks, blk_src, blk_dst, reward, horizon):
    blocks = gen_blocks[0, 0]
    src = blk_src[0, 0]
    dst = blk_dst[0, 0]
    span = x_init.shape[0]
    ny, nzl = SHAPE[0], SHAPE[1]
    rows = ny * nzl
    weights = poisson_weights(horizon)
    reward_f = reward.astype(jnp.float32)[:, None, :]
    moves = [(dy, dzl) for dy in range(ny) for dzl in range(nzl)]
    y, zl = lax.axis_index("y"), lax.axis_index("zl")
    order = jnp.stack([(y + dy) % ny * nzl + (zl + dzl) % nzl for dy, dzl in moves]).astype(jnp.int32)
    state = x_init
    accumulated = weights[0] * reward_f * state
    for iteration in range(STEPS):
        rounded = state.astype(jnp.bfloat16)
        whole = lax.all_gather(rounded, COL, axis=0, tiled=True)
        own, *sends = products(src, dst, order, whole, blocks, rows, span)
        mine = own
        for (dy, dzl), send in zip(moves[1:], sends):
            mine = mine + lax.ppermute(send, ROW, shifted(dy, dzl)).astype(jnp.float32)
        state = state + mine
        accumulated = accumulated + weights[iteration + 1] * reward_f * state
    return (state, accumulated)


def solution(mesh):
    fine = Mesh(mesh.devices.reshape(SHAPE), AXES)
    rc = P((*ROW, *COL), None, None)
    in_specs = (
        rc,
        P(ROW, COL, None, None, None),
        P(ROW, COL, None),
        P(ROW, COL, None),
        P((*ROW, *COL), None),
        P(),
    )
    return jax.shard_map(shards, mesh=fine, in_specs=in_specs, out_specs=(rc, rc), check_vma=False)
```

```python
import jax
import jax.numpy as jnp
from jax import lax
from jax.experimental import pallas as pl
from jax.experimental.pallas import tpu as pltpu
from jax.sharding import Mesh, PartitionSpec as P

STEPS = 3
AXES = ("y", "zl", "x", "zh", "core")
SHAPE = (4, 2, 4, 4, 2)
ROW = ("y", "zl")
COL = ("x", "zh", "core")
GROUPS = 8
TURNS = (0, 1, 3, 2)


def poisson_weights(horizon):
    rate_time = horizon[0]
    poisson_term = jnp.exp(-rate_time)
    cumulated = poisson_term
    weights = [(1.0 - cumulated) / rate_time]
    for iteration in range(STEPS):
        poisson_term = poisson_term * rate_time / (iteration + 1.0)
        cumulated = cumulated + poisson_term
        weights.append((1.0 - cumulated) / rate_time)
    return weights


def add_products(step, base, src, dst, x_ref, blk_ref, acc):
    slots = blk_ref.shape[0]
    for slot in range(slots):
        at = step * slots + slot
        vectors = x_ref[src[at] - base]
        into = dst[at]
        acc[into] += jnp.dot(vectors, blk_ref[slot], preferred_element_type=jnp.float32)


def hand_out(place, own_ref, send_ref, acc):
    span = own_ref.shape[0]
    mine = pl.ds(place[0] * span, span)
    own_ref[...] = acc[mine]
    send_ref[...] = acc[...].astype(send_ref.dtype)
    send_ref[mine] = jnp.zeros(own_ref.shape, send_ref.dtype)


def whole_body(src, dst, place, x_ref, blk_ref, own_ref, send_ref, acc):
    step = pl.program_id(0)

    @pl.when(step == 0)
    def _():
        acc[...] = jnp.zeros_like(acc)

    add_products(step, step * x_ref.shape[0], src, dst, x_ref, blk_ref, acc)

    @pl.when(step == pl.num_programs(0) - 1)
    def _():
        hand_out(place, own_ref, send_ref, acc)


def pieces_body(src, dst, place, *refs):
    pieces, (blk_ref, own_ref, send_ref, acc, whole, sems) = refs[:8], refs[8:]
    span = own_ref.shape[0]
    step = pl.program_id(0)

    @pl.when(step == 0)
    def _():
        copies = []
        for core in range(2):
            for at_x in range(4):
                for at_z in range(4):
                    shard = len(copies)
                    copies.append(
                        pltpu.make_async_copy(
                            pieces[core * 4 + at_x].at[pl.ds(at_z * span, span)],
                            whole.at[pl.ds(place[1 + shard] * span, span)],
                            sems.at[shard],
                        )
                    )
        for copy in copies:
            copy.start()
        acc[...] = jnp.zeros_like(acc)
        for copy in copies:
            copy.wait()

    add_products(step, 0, src, dst, whole, blk_ref, acc)

    @pl.when(step == pl.num_programs(0) - 1)
    def _():
        hand_out(place, own_ref, send_ref, acc)


def products(src, dst, place, given, blocks, span):
    n, block_len, _ = blocks.shape
    configs = given[0].shape[1]
    targets = SHAPE[0] * SHAPE[1] * span
    sources = SHAPE[2] * SHAPE[3] * SHAPE[4] * span
    piece = (span, configs, block_len)
    send = (targets, configs, block_len)
    scratch = [pltpu.VMEM(send, jnp.float32)]
    if len(given) == 1:
        body = whole_body
        specs = [pl.BlockSpec((sources // GROUPS, configs, block_len), lambda i, *_: (i, 0, 0))]
    else:
        body = pieces_body
        specs = [pl.BlockSpec(memory_space=pl.ANY)] * len(given)
        scratch += [pltpu.VMEM((sources, configs, block_len), jnp.bfloat16), pltpu.SemaphoreType.DMA((32,))]
    return pl.pallas_call(
        body,
        out_shape=[jax.ShapeDtypeStruct(piece, jnp.float32), jax.ShapeDtypeStruct(send, jnp.bfloat16)],
        grid_spec=pltpu.PrefetchScalarGridSpec(
            num_scalar_prefetch=3,
            grid=(GROUPS,),
            in_specs=specs + [pl.BlockSpec((n // GROUPS, block_len, block_len), lambda i, *_: (i, 0, 0))],
            out_specs=[pl.BlockSpec(piece, lambda i, *_: (0, 0, 0)), pl.BlockSpec(send, lambda i, *_: (0, 0, 0))],
            scratch_shapes=scratch,
        ),
        compiler_params=pltpu.CompilerParams(vmem_limit_bytes=32 << 20),
        cost_estimate=pl.CostEstimate(
            flops=2 * n * configs * block_len * block_len,
            bytes_accessed=2 * (sources * configs * block_len + blocks.size + targets * configs * block_len),
            transcendentals=0,
        ),
        name="products",
    )(src, dst, place, *given, blocks)


def turn(value, axis, by):
    n = lax.axis_size(axis)
    return lax.ppermute(value, axis, [(i, (i + by) % n) for i in range(n)])


def after(value, *others):
    return lax.optimization_barrier((value, *others))[0]


def spread_z(mine):
    return [turn(mine, "zh", by) for by in TURNS[1:]]


def spread_x(mine, from_z):
    column = jnp.concatenate([mine, *from_z], axis=0)
    return [column] + [turn(column, "x", by) for by in TURNS[1:]]


def reduce_rows(own, send):
    got = lax.all_to_all(send, ROW, 0, 0, tiled=True)
    got = got.reshape(SHAPE[0] * SHAPE[1], *own.shape).astype(jnp.float32)
    return own + jnp.sum(got, axis=0)


def shards(x_init, gen_blocks, blk_src, blk_dst, reward, horizon):
    blocks = gen_blocks[0, 0]
    src = blk_src[0, 0]
    dst = blk_dst[0, 0]
    span = x_init.shape[0]
    half = x_init.shape[1] // 2
    weights = poisson_weights(horizon)
    reward_f = reward.astype(jnp.float32)[:, None, :]
    x, zh, core = (lax.axis_index(a) for a in COL)
    row = lax.axis_index("y") * SHAPE[1] + lax.axis_index("zl")
    place = [row]
    for other in range(2):
        for by_x in TURNS:
            for by_z in TURNS:
                place.append((((x - by_x) % 4) * 4 + (zh - by_z) % 4) * 2 + (core + other) % 2)
    place = jnp.stack(place).astype(jnp.int32)
    state_a, state_b = x_init[:, :half], x_init[:, half:]
    sum_a = weights[0] * reward_f * state_a
    sum_b = weights[0] * reward_f * state_b
    for iteration in range(STEPS):
        low_a = state_a.astype(jnp.bfloat16)
        low_b = state_b.astype(jnp.bfloat16)
        whole = lax.all_gather(low_a, COL, axis=0, tiled=True)
        near = spread_x(low_b, spread_z(low_b))
        far = [turn(piece, "core", 1) for piece in near]
        state_b = state_b + reduce_rows(*products(src, dst, place, near + far, blocks, span))
        state_a = state_a + reduce_rows(*products(src, dst, place, [whole], blocks, span))
        sum_a = sum_a + weights[iteration + 1] * reward_f * state_a
        sum_b = sum_b + weights[iteration + 1] * reward_f * state_b
    return (
        jnp.concatenate([state_a, state_b], axis=1),
        jnp.concatenate([sum_a, sum_b], axis=1),
    )


def solution(mesh):
    fine = Mesh(mesh.devices.reshape(SHAPE), AXES)
    rc = P((*ROW, *COL), None, None)
    in_specs = (
        rc,
        P(ROW, COL, None, None, None),
        P(ROW, COL, None),
        P(ROW, COL, None),
        P((*ROW, *COL), None),
        P(),
    )
    return jax.shard_map(shards, mesh=fine, in_specs=in_specs, out_specs=(rc, rc), check_vma=False)
```

```python
import jax
import jax.numpy as jnp
from jax import lax
from jax.experimental import pallas as pl
from jax.experimental.pallas import tpu as pltpu
from jax.sharding import Mesh, PartitionSpec as P

STEPS = 3
AXES = ("y", "zl", "x", "zh", "core")
SHAPE = (4, 2, 4, 4, 2)
ROW = ("y", "zl")
COL = ("x", "zh", "core")
GROUPS = 8
TURNS = (0, 1, 3, 2)


def poisson_weights(horizon):
    rate_time = horizon[0]
    poisson_term = jnp.exp(-rate_time)
    cumulated = poisson_term
    weights = [(1.0 - cumulated) / rate_time]
    for iteration in range(STEPS):
        poisson_term = poisson_term * rate_time / (iteration + 1.0)
        cumulated = cumulated + poisson_term
        weights.append((1.0 - cumulated) / rate_time)
    return weights


def add_products(step, base, src, dst, x_ref, blk_ref, acc):
    slots = blk_ref.shape[0]
    for slot in range(slots):
        at = step * slots + slot
        vectors = x_ref[src[at] - base]
        into = dst[at]
        acc[into] += jnp.dot(vectors, blk_ref[slot], preferred_element_type=jnp.float32)


def hand_out(place, own_ref, send_ref, acc):
    span = own_ref.shape[0]
    mine = pl.ds(place[0] * span, span)
    own_ref[...] = acc[mine]
    send_ref[...] = acc[...].astype(send_ref.dtype)
    send_ref[mine] = jnp.zeros(own_ref.shape, send_ref.dtype)


def whole_body(src, dst, place, x_ref, blk_ref, own_ref, send_ref, acc):
    step = pl.program_id(0)

    @pl.when(step == 0)
    def _():
        acc[...] = jnp.zeros_like(acc)

    add_products(step, step * x_ref.shape[0], src, dst, x_ref, blk_ref, acc)

    @pl.when(step == pl.num_programs(0) - 1)
    def _():
        hand_out(place, own_ref, send_ref, acc)


def pieces_body(src, dst, place, *refs):
    pieces, (blk_ref, own_ref, send_ref, acc, whole, sems) = refs[:8], refs[8:]
    span = own_ref.shape[0]
    step = pl.program_id(0)

    @pl.when(step == 0)
    def _():
        copies = []
        for core in range(2):
            for at_x in range(4):
                for at_z in range(4):
                    shard = len(copies)
                    copies.append(
                        pltpu.make_async_copy(
                            pieces[core * 4 + at_x].at[pl.ds(at_z * span, span)],
                            whole.at[pl.ds(place[1 + shard] * span, span)],
                            sems.at[shard],
                        )
                    )
        for copy in copies:
            copy.start()
        acc[...] = jnp.zeros_like(acc)
        for copy in copies:
            copy.wait()

    add_products(step, 0, src, dst, whole, blk_ref, acc)

    @pl.when(step == pl.num_programs(0) - 1)
    def _():
        hand_out(place, own_ref, send_ref, acc)


def products(src, dst, place, given, blocks, span):
    n, block_len, _ = blocks.shape
    configs = given[0].shape[1]
    targets = SHAPE[0] * SHAPE[1] * span
    sources = SHAPE[2] * SHAPE[3] * SHAPE[4] * span
    piece = (span, configs, block_len)
    send = (targets, configs, block_len)
    scratch = [pltpu.VMEM(send, jnp.float32)]
    if len(given) == 1:
        body = whole_body
        specs = [pl.BlockSpec((sources // GROUPS, configs, block_len), lambda i, *_: (i, 0, 0))]
    else:
        body = pieces_body
        specs = [pl.BlockSpec(memory_space=pl.ANY)] * len(given)
        scratch += [pltpu.VMEM((sources, configs, block_len), jnp.bfloat16), pltpu.SemaphoreType.DMA((32,))]
    return pl.pallas_call(
        body,
        out_shape=[jax.ShapeDtypeStruct(piece, jnp.float32), jax.ShapeDtypeStruct(send, jnp.bfloat16)],
        grid_spec=pltpu.PrefetchScalarGridSpec(
            num_scalar_prefetch=3,
            grid=(GROUPS,),
            in_specs=specs + [pl.BlockSpec((n // GROUPS, block_len, block_len), lambda i, *_: (i, 0, 0))],
            out_specs=[pl.BlockSpec(piece, lambda i, *_: (0, 0, 0)), pl.BlockSpec(send, lambda i, *_: (0, 0, 0))],
            scratch_shapes=scratch,
        ),
        compiler_params=pltpu.CompilerParams(vmem_limit_bytes=60 << 20),
        cost_estimate=pl.CostEstimate(
            flops=2 * n * configs * block_len * block_len,
            bytes_accessed=2 * (sources * configs * block_len + blocks.size + targets * configs * block_len),
            transcendentals=0,
        ),
        name="products",
    )(src, dst, place, *given, blocks)


def turn(value, axis, by):
    n = lax.axis_size(axis)
    return lax.ppermute(value, axis, [(i, (i + by) % n) for i in range(n)])


def after(values, *others):
    return lax.optimization_barrier((values, others))[0]


def spread_x(mine):
    column = jnp.concatenate([mine] + [turn(mine, "zh", by) for by in TURNS[1:]], axis=0)
    return [column] + [turn(column, "x", by) for by in TURNS[1:]]


def reduce_rows(own, send):
    got = lax.all_to_all(send, ROW, 0, 0, tiled=True)
    got = got.reshape(SHAPE[0] * SHAPE[1], *own.shape).astype(jnp.float32)
    return own + jnp.sum(got, axis=0)


def shards(x_init, gen_blocks, blk_src, blk_dst, reward, horizon):
    blocks = gen_blocks[0, 0]
    src = blk_src[0, 0]
    dst = blk_dst[0, 0]
    span = x_init.shape[0]
    half = x_init.shape[1] // 2
    weights = poisson_weights(horizon)
    reward_f = reward.astype(jnp.float32)[:, None, :]
    x, zh, core = (lax.axis_index(a) for a in COL)
    row = lax.axis_index("y") * SHAPE[1] + lax.axis_index("zl")
    place = [row]
    for other in range(2):
        for by_x in TURNS:
            for by_z in TURNS:
                place.append((((x - by_x) % 4) * 4 + (zh - by_z) % 4) * 2 + (core + other) % 2)
    place = jnp.stack(place).astype(jnp.int32)
    state_a, state_b = x_init[:, :half], x_init[:, half:]
    sum_a = weights[0] * reward_f * state_a
    sum_b = weights[0] * reward_f * state_b
    near = spread_x(state_b.astype(jnp.bfloat16))
    whole = lax.all_gather(state_a.astype(jnp.bfloat16), COL, axis=0, tiled=True)
    for iteration in range(STEPS):
        far = [turn(piece, "core", 1) for piece in near]
        state_b = state_b + reduce_rows(*products(src, dst, place, near + far, blocks, span))
        sum_b = sum_b + weights[iteration + 1] * reward_f * state_b
        if iteration + 1 < STEPS:
            near = spread_x(state_b.astype(jnp.bfloat16))
            whole = after(whole, near[0])
        state_a = state_a + reduce_rows(*products(src, dst, place, [whole], blocks, span))
        sum_a = sum_a + weights[iteration + 1] * reward_f * state_a
        if iteration + 1 < STEPS:
            low_a = state_a.astype(jnp.bfloat16)
            low_a, *near = lax.optimization_barrier((low_a, *near))
            whole = lax.all_gather(low_a, COL, axis=0, tiled=True)
    return (
        jnp.concatenate([state_a, state_b], axis=1),
        jnp.concatenate([sum_a, sum_b], axis=1),
    )


def solution(mesh):
    fine = Mesh(mesh.devices.reshape(SHAPE), AXES)
    rc = P((*ROW, *COL), None, None)
    in_specs = (
        rc,
        P(ROW, COL, None, None, None),
        P(ROW, COL, None),
        P(ROW, COL, None),
        P((*ROW, *COL), None),
        P(),
    )
    return jax.shard_map(shards, mesh=fine, in_specs=in_specs, out_specs=(rc, rc), check_vma=False)
```

```python
import jax
import jax.numpy as jnp
from jax import lax
from jax.experimental import pallas as pl
from jax.experimental.pallas import tpu as pltpu
from jax.sharding import Mesh, PartitionSpec as P

STEPS = 3
AXES = ("y", "zl", "x", "zh", "core")
SHAPE = (4, 2, 4, 4, 2)
ROW = ("y", "zl")
COL = ("x", "zh", "core")
GROUPS = 8
STREAMS = 4
TURNS = (0, 1, 3, 2)


def poisson_weights(horizon):
    rate_time = horizon[0]
    poisson_term = jnp.exp(-rate_time)
    cumulated = poisson_term
    weights = [(1.0 - cumulated) / rate_time]
    for iteration in range(STEPS):
        poisson_term = poisson_term * rate_time / (iteration + 1.0)
        cumulated = cumulated + poisson_term
        weights.append((1.0 - cumulated) / rate_time)
    return weights


def add_products(step, base, src, dst, x_ref, streams, acc):
    slots = streams[0].shape[0]
    for slot in range(len(streams) * slots):
        at = step * len(streams) * slots + slot
        vectors = x_ref[src[at] - base]
        into = dst[at]
        block = streams[slot // slots][slot % slots]
        acc[into] += jnp.dot(vectors, block, preferred_element_type=jnp.float32)


def hand_out(place, own_ref, send_ref, acc):
    span = own_ref.shape[0]
    mine = pl.ds(place[0] * span, span)
    own_ref[...] = acc[mine]
    send_ref[...] = acc[...].astype(send_ref.dtype)
    send_ref[mine] = jnp.zeros(own_ref.shape, send_ref.dtype)


def whole_body(src, dst, place, x_ref, *refs):
    streams, (own_ref, send_ref, acc) = refs[:STREAMS], refs[STREAMS:]
    step = pl.program_id(0)

    @pl.when(step == 0)
    def _():
        acc[...] = jnp.zeros_like(acc)

    add_products(step, step * x_ref.shape[0], src, dst, x_ref, streams, acc)

    @pl.when(step == pl.num_programs(0) - 1)
    def _():
        hand_out(place, own_ref, send_ref, acc)


def pieces_body(src, dst, place, *refs):
    pieces, streams = refs[:8], refs[8 : 8 + STREAMS]
    own_ref, send_ref, acc, whole, sems = refs[8 + STREAMS :]
    span = own_ref.shape[0]
    step = pl.program_id(0)

    @pl.when(step == 0)
    def _():
        copies = []
        for core in range(2):
            for at_x in range(4):
                for at_z in range(4):
                    shard = len(copies)
                    copies.append(
                        pltpu.make_async_copy(
                            pieces[core * 4 + at_x].at[pl.ds(at_z * span, span)],
                            whole.at[pl.ds(place[1 + shard] * span, span)],
                            sems.at[shard],
                        )
                    )
        for copy in copies:
            copy.start()
        acc[...] = jnp.zeros_like(acc)
        for copy in copies:
            copy.wait()

    add_products(step, 0, src, dst, whole, streams, acc)

    @pl.when(step == pl.num_programs(0) - 1)
    def _():
        hand_out(place, own_ref, send_ref, acc)


def stream(n, block_len, q):
    shape = (n // GROUPS // STREAMS, block_len, block_len)
    return pl.BlockSpec(shape, lambda i, *_: (i * STREAMS + q, 0, 0))


def products(src, dst, place, given, blocks, span):
    n, block_len, _ = blocks.shape
    configs = given[0].shape[1]
    targets = SHAPE[0] * SHAPE[1] * span
    sources = SHAPE[2] * SHAPE[3] * SHAPE[4] * span
    piece = (span, configs, block_len)
    send = (targets, configs, block_len)
    scratch = [pltpu.VMEM(send, jnp.float32)]
    if len(given) == 1:
        body = whole_body
        specs = [pl.BlockSpec((sources // GROUPS, configs, block_len), lambda i, *_: (i, 0, 0))]
    else:
        body = pieces_body
        specs = [pl.BlockSpec(memory_space=pl.ANY)] * len(given)
        scratch += [pltpu.VMEM((sources, configs, block_len), jnp.bfloat16), pltpu.SemaphoreType.DMA((32,))]
    return pl.pallas_call(
        body,
        out_shape=[jax.ShapeDtypeStruct(piece, jnp.float32), jax.ShapeDtypeStruct(send, jnp.bfloat16)],
        grid_spec=pltpu.PrefetchScalarGridSpec(
            num_scalar_prefetch=3,
            grid=(GROUPS,),
            in_specs=specs + [stream(n, block_len, q) for q in range(STREAMS)],
            out_specs=[pl.BlockSpec(piece, lambda i, *_: (0, 0, 0)), pl.BlockSpec(send, lambda i, *_: (0, 0, 0))],
            scratch_shapes=scratch,
        ),
        compiler_params=pltpu.CompilerParams(vmem_limit_bytes=60 << 20),
        cost_estimate=pl.CostEstimate(
            flops=2 * n * configs * block_len * block_len,
            bytes_accessed=2 * (sources * configs * block_len + blocks.size + targets * configs * block_len),
            transcendentals=0,
        ),
        name="products",
    )(src, dst, place, *given, *[blocks] * STREAMS)


def turn(value, axis, by):
    n = lax.axis_size(axis)
    return lax.ppermute(value, axis, [(i, (i + by) % n) for i in range(n)])


def after(values, *others):
    return lax.optimization_barrier((values, others))[0]


def spread_x(mine):
    column = jnp.concatenate([mine] + [turn(mine, "zh", by) for by in TURNS[1:]], axis=0)
    return [column] + [turn(column, "x", by) for by in TURNS[1:]]


def reduce_rows(own, send):
    got = lax.all_to_all(send, ROW, 0, 0, tiled=True)
    got = got.reshape(SHAPE[0] * SHAPE[1], *own.shape).astype(jnp.float32)
    return own + jnp.sum(got, axis=0)


def shards(x_init, gen_blocks, blk_src, blk_dst, reward, horizon):
    blocks = gen_blocks[0, 0]
    src = blk_src[0, 0]
    dst = blk_dst[0, 0]
    span = x_init.shape[0]
    half = x_init.shape[1] // 2
    weights = poisson_weights(horizon)
    reward_f = reward.astype(jnp.float32)[:, None, :]
    x, zh, core = (lax.axis_index(a) for a in COL)
    row = lax.axis_index("y") * SHAPE[1] + lax.axis_index("zl")
    place = [row]
    for other in range(2):
        for by_x in TURNS:
            for by_z in TURNS:
                place.append((((x - by_x) % 4) * 4 + (zh - by_z) % 4) * 2 + (core + other) % 2)
    place = jnp.stack(place).astype(jnp.int32)
    state_a, state_b = x_init[:, :half], x_init[:, half:]
    sum_a = weights[0] * reward_f * state_a
    sum_b = weights[0] * reward_f * state_b
    near = spread_x(state_b.astype(jnp.bfloat16))
    whole = lax.all_gather(state_a.astype(jnp.bfloat16), COL, axis=0, tiled=True)
    for iteration in range(STEPS):
        last = iteration + 1 == STEPS
        own_a, send_a = products(src, dst, place, [after(whole, *near)], blocks, span)
        near = after(near, send_a)
        far = [turn(piece, "core", 1) for piece in near]
        own_b, send_b = products(src, dst, place, near + far, blocks, span)
        state_a = state_a + reduce_rows(own_a, send_a)
        sum_a = sum_a + weights[iteration + 1] * reward_f * state_a
        if not last:
            low_a = state_a.astype(jnp.bfloat16)
            low_a, send_b = lax.optimization_barrier((low_a, send_b))
            whole = lax.all_gather(low_a, COL, axis=0, tiled=True)
        state_b = state_b + reduce_rows(own_b, send_b)
        sum_b = sum_b + weights[iteration + 1] * reward_f * state_b
        if not last:
            near = spread_x(state_b.astype(jnp.bfloat16))
    return (
        jnp.concatenate([state_a, state_b], axis=1),
        jnp.concatenate([sum_a, sum_b], axis=1),
    )


def solution(mesh):
    fine = Mesh(mesh.devices.reshape(SHAPE), AXES)
    rc = P((*ROW, *COL), None, None)
    in_specs = (
        rc,
        P(ROW, COL, None, None, None),
        P(ROW, COL, None),
        P(ROW, COL, None),
        P((*ROW, *COL), None),
        P(),
    )
    return jax.shard_map(shards, mesh=fine, in_specs=in_specs, out_specs=(rc, rc), check_vma=False)
```

```python
import jax
import jax.numpy as jnp
from jax import lax
from jax.experimental import pallas as pl
from jax.experimental.pallas import tpu as pltpu
from jax.sharding import Mesh, PartitionSpec as P

STEPS = 3
AXES = ("y", "zl", "x", "zh", "core")
SHAPE = (4, 2, 4, 4, 2)
ROW = ("y", "zl")
COL = ("x", "zh", "core")
GROUPS = 8
AHEAD = 3
TURNS = (0, 1, 3, 2)


def poisson_weights(horizon):
    rate_time = horizon[0]
    poisson_term = jnp.exp(-rate_time)
    cumulated = poisson_term
    weights = [(1.0 - cumulated) / rate_time]
    for iteration in range(STEPS):
        poisson_term = poisson_term * rate_time / (iteration + 1.0)
        cumulated = cumulated + poisson_term
        weights.append((1.0 - cumulated) / rate_time)
    return weights


def hand_out(place, own_ref, send_ref, acc):
    span = own_ref.shape[0]
    mine = pl.ds(place[0] * span, span)
    own_ref[...] = acc[mine]
    send_ref[...] = acc[...].astype(send_ref.dtype)
    send_ref[mine] = jnp.zeros(own_ref.shape, send_ref.dtype)


def whole_body(src, dst, place, given, blk, own_ref, send_ref, acc, held, sems, whole, more_sems):
    slots = held.shape[0] // GROUPS
    rows = whole.shape[0] // GROUPS

    def fetch(group):
        part = pl.ds(pl.multiple_of(group * rows, rows), rows)
        block = pl.ds(pl.multiple_of(group * slots, slots), slots)
        return (
            pltpu.make_async_copy(given.at[part], whole.at[part], more_sems.at[group]),
            pltpu.make_async_copy(blk.at[block], held.at[block], sems.at[group]),
        )

    for group in range(AHEAD):
        for copy in fetch(group):
            copy.start()
    acc[...] = jnp.zeros_like(acc)

    @pl.loop(0, GROUPS)
    def _(group):
        for copy in fetch(group):
            copy.wait()

        @pl.when(group + AHEAD < GROUPS)
        def _():
            for copy in fetch(group + AHEAD):
                copy.start()

        for slot in range(slots):
            at = group * slots + slot
            acc[dst[at]] += jnp.dot(whole[src[at]], held[at], preferred_element_type=jnp.float32)

    hand_out(place, own_ref, send_ref, acc)


def pieces_body(src, dst, place, *refs):
    pieces, (blk, own_ref, send_ref, acc, held, sems) = refs[:-6], refs[-6:]
    span = own_ref.shape[0]
    counts = [piece.shape[0] // span for piece in pieces]
    firsts = [sum(counts[:number]) for number in range(len(counts))]
    slots = held.shape[0] // sum(counts)

    def fetch(shard):
        there = pl.ds(pl.multiple_of(shard * slots, slots), slots)
        part = pl.ds(pl.multiple_of(place[1 + shard] * slots, slots), slots)
        return pltpu.make_async_copy(blk.at[part], held.at[there], sems.at[shard])

    ahead = 4 * AHEAD
    for shard in range(ahead):
        fetch(shard).start()
    acc[...] = jnp.zeros_like(acc)
    for first, count, piece in zip(firsts, counts, pieces):

        @pl.loop(0, count // 2)
        def _(pair):
            for one in range(2):
                at_z = pair * 2 + one
                fetch(first + at_z).wait()

                @pl.when(first + at_z + ahead < sum(counts))
                def _():
                    fetch(first + at_z + ahead).start()

                shard = place[1 + first + at_z]
                for slot in range(slots):
                    at = shard * slots + slot
                    row = src[at] + (at_z - shard) * span
                    block = held[(first + at_z) * slots + slot]
                    acc[dst[at]] += jnp.dot(piece[row], block, preferred_element_type=jnp.float32)

    hand_out(place, own_ref, send_ref, acc)


def products(src, dst, place, given, blocks, span):
    n, block_len, _ = blocks.shape
    configs = given[0].shape[1]
    targets = SHAPE[0] * SHAPE[1] * span
    sources = SHAPE[2] * SHAPE[3] * SHAPE[4] * span
    piece = (span, configs, block_len)
    send = (targets, configs, block_len)
    scratch = [pltpu.VMEM(send, jnp.float32), pltpu.VMEM(blocks.shape, blocks.dtype)]
    if len(given) == 1:
        body, where = whole_body, pltpu.HBM
        scratch += [pltpu.SemaphoreType.DMA((GROUPS,)), pltpu.VMEM((sources, configs, block_len), jnp.bfloat16)]
        scratch += [pltpu.SemaphoreType.DMA((GROUPS,))]
    else:
        body, where = pieces_body, pltpu.VMEM
        scratch += [pltpu.SemaphoreType.DMA((sources // span,))]
    given = [pltpu.with_memory_space_constraint(value, where) for value in given]
    blocks = pltpu.with_memory_space_constraint(blocks, pltpu.HBM)
    return pl.pallas_call(
        body,
        out_shape=[jax.ShapeDtypeStruct(piece, jnp.float32), jax.ShapeDtypeStruct(send, jnp.bfloat16)],
        grid_spec=pltpu.PrefetchScalarGridSpec(
            num_scalar_prefetch=3,
            grid=(1,),
            in_specs=[pl.BlockSpec(memory_space=where)] * len(given) + [pl.BlockSpec(memory_space=pltpu.HBM)],
            out_specs=[pl.BlockSpec(piece, lambda i, *_: (0, 0, 0)), pl.BlockSpec(send, lambda i, *_: (0, 0, 0))],
            scratch_shapes=scratch,
        ),
        compiler_params=pltpu.CompilerParams(vmem_limit_bytes=24 << 20),
        cost_estimate=pl.CostEstimate(
            flops=2 * n * configs * block_len * block_len,
            bytes_accessed=2 * (sources * configs * block_len + n * block_len * block_len),
            transcendentals=0,
        ),
        name="products",
    )(src, dst, place, *given, blocks)


def turn(value, axis, by):
    n = lax.axis_size(axis)
    return lax.ppermute(value, axis, [(i, (i + by) % n) for i in range(n)])


def after(values, *others):
    return lax.optimization_barrier((values, others))[0]


def spread_z(mine):
    return [mine] + [turn(mine, "zh", by) for by in TURNS[1:]]


def spread_x(column):
    return [column, turn(column, "x", 1), turn(column, "x", 3)]


def pass_on(near):
    half = near[0].shape[0] // 2
    near = near + [turn(near[1][:half], "x", 1), turn(near[2][half:], "x", 3)]
    return jnp.concatenate(near, axis=0)


def exchange_rows(send):
    return lax.all_to_all(send, ROW, 0, 0, tiled=True)


def add_rows(own, got):
    total = own
    for part in jnp.split(got, SHAPE[0] * SHAPE[1], axis=0):
        total = total + part.astype(jnp.float32)
    return total


def shards(x_init, gen_blocks, blk_src, blk_dst, reward, horizon):
    blocks = gen_blocks[0, 0]
    src = blk_src[0, 0]
    dst = blk_dst[0, 0]
    span = x_init.shape[0]
    half = x_init.shape[1] // 2
    weights = poisson_weights(horizon)
    reward_f = reward.astype(jnp.float32)[:, None, :]
    x, zh, core = (lax.axis_index(a) for a in COL)
    row = lax.axis_index("y") * SHAPE[1] + lax.axis_index("zl")
    place = [row]
    for other in range(2):
        for by_x in TURNS:
            for by_z in TURNS:
                place.append((((x - by_x) % 4) * 4 + (zh - by_z) % 4) * 2 + (core + other) % 2)
    place = jnp.stack(place).astype(jnp.int32)
    state_a, state_b = x_init[:, :half], x_init[:, half:]
    sum_a = weights[0] * reward_f * state_a
    sum_b = weights[0] * reward_f * state_b
    whole = lax.all_gather(state_a.astype(jnp.bfloat16), COL, axis=0, tiled=True)
    column = jnp.concatenate(spread_z(state_b.astype(jnp.bfloat16)), axis=0)
    near = spread_x(column)
    for iteration in range(STEPS):
        last = iteration + 1 == STEPS
        near = pass_on(near)
        own_b, send_b = products(src, dst, place, [near, turn(near, "core", 1)], blocks, span)
        state_b = state_b + add_rows(own_b, exchange_rows(send_b))
        sum_b = sum_b + weights[iteration + 1] * reward_f * state_b
        low_b = state_b.astype(jnp.bfloat16)
        whole = after(whole, low_b if iteration == 1 else send_b)
        own_a, send_a = products(src, dst, place, [whole], blocks, span)
        got_a = exchange_rows(send_a)
        if not last:
            column = jnp.concatenate(after(spread_z(low_b), send_a), axis=0)
            got_a = after(got_a, column)
        state_a = state_a + add_rows(own_a, got_a)
        sum_a = sum_a + weights[iteration + 1] * reward_f * state_a
        if not last:
            low_a = state_a.astype(jnp.bfloat16)
            whole = lax.all_gather(low_a, COL, axis=0, tiled=True)
            near = after(spread_x(column), low_a)
    return (
        jnp.concatenate([state_a, state_b], axis=1),
        jnp.concatenate([sum_a, sum_b], axis=1),
    )


def solution(mesh):
    fine = Mesh(mesh.devices.reshape(SHAPE), AXES)
    rc = P((*ROW, *COL), None, None)
    in_specs = (
        rc,
        P(ROW, COL, None, None, None),
        P(ROW, COL, None),
        P(ROW, COL, None),
        P((*ROW, *COL), None),
        P(),
    )
    return jax.shard_map(shards, mesh=fine, in_specs=in_specs, out_specs=(rc, rc), check_vma=False)
```

```python
import jax
import jax.numpy as jnp
from jax import lax
from jax.experimental import pallas as pl
from jax.experimental.pallas import tpu as pltpu
from jax.sharding import Mesh, PartitionSpec as P

STEPS = 3
AXES = ("y", "zl", "x", "zh", "core")
SHAPE = (4, 2, 4, 4, 2)
ROW = ("y", "zl")
COL = ("x", "zh", "core")
GROUPS = 8
AHEAD = 3
TURNS = (0, 1, 3, 2)


def poisson_weights(horizon):
    rate_time = horizon[0]
    poisson_term = jnp.exp(-rate_time)
    cumulated = poisson_term
    weights = [(1.0 - cumulated) / rate_time]
    for iteration in range(STEPS):
        poisson_term = poisson_term * rate_time / (iteration + 1.0)
        cumulated = cumulated + poisson_term
        weights.append((1.0 - cumulated) / rate_time)
    return weights


def hand_out(place, own_ref, send_ref, acc):
    span = own_ref.shape[0]
    mine = pl.ds(place[0] * span, span)
    own_ref[...] = acc[mine]
    send_ref[...] = acc[...].astype(send_ref.dtype)
    send_ref[mine] = jnp.zeros(own_ref.shape, send_ref.dtype)


def whole_body(src, dst, place, given, blk, own_ref, send_ref, acc, held, sems, whole, more_sems):
    slots = held.shape[0] // GROUPS
    rows = whole.shape[0] // GROUPS

    def fetch(group):
        part = pl.ds(pl.multiple_of(group * rows, rows), rows)
        block = pl.ds(pl.multiple_of(group * slots, slots), slots)
        return (
            pltpu.make_async_copy(given.at[part], whole.at[part], more_sems.at[group]),
            pltpu.make_async_copy(blk.at[block], held.at[block], sems.at[group]),
        )

    for group in range(AHEAD):
        for copy in fetch(group):
            copy.start()
    acc[...] = jnp.zeros_like(acc)

    @pl.loop(0, GROUPS)
    def _(group):
        for copy in fetch(group):
            copy.wait()

        @pl.when(group + AHEAD < GROUPS)
        def _():
            for copy in fetch(group + AHEAD):
                copy.start()

        for slot in range(slots):
            at = group * slots + slot
            acc[dst[at]] += jnp.dot(whole[src[at]], held[at], preferred_element_type=jnp.float32)

    hand_out(place, own_ref, send_ref, acc)


def pieces_body(src, dst, place, *refs):
    pieces, (blk, own_ref, send_ref, acc, held, sems) = refs[:-6], refs[-6:]
    span = own_ref.shape[0]
    counts = [piece.shape[0] // span for piece in pieces]
    firsts = [sum(counts[:number]) for number in range(len(counts))]
    slots = held.shape[0] // sum(counts)

    def fetch(shard):
        there = pl.ds(pl.multiple_of(shard * slots, slots), slots)
        part = pl.ds(pl.multiple_of(place[1 + shard] * slots, slots), slots)
        return pltpu.make_async_copy(blk.at[part], held.at[there], sems.at[shard])

    ahead = 4 * AHEAD
    for shard in range(ahead):
        fetch(shard).start()
    acc[...] = jnp.zeros_like(acc)
    for first, count, piece in zip(firsts, counts, pieces):

        @pl.loop(0, count // 2)
        def _(pair):
            for one in range(2):
                at_z = pair * 2 + one
                fetch(first + at_z).wait()

                @pl.when(first + at_z + ahead < sum(counts))
                def _():
                    fetch(first + at_z + ahead).start()

                shard = place[1 + first + at_z]
                for slot in range(slots):
                    at = shard * slots + slot
                    row = src[at] + (at_z - shard) * span
                    block = held[(first + at_z) * slots + slot]
                    acc[dst[at]] += jnp.dot(piece[row], block, preferred_element_type=jnp.float32)

    hand_out(place, own_ref, send_ref, acc)


def products(src, dst, place, given, blocks, span):
    n, block_len, _ = blocks.shape
    configs = given[0].shape[1]
    targets = SHAPE[0] * SHAPE[1] * span
    sources = SHAPE[2] * SHAPE[3] * SHAPE[4] * span
    piece = (span, configs, block_len)
    send = (targets, configs, block_len)
    scratch = [pltpu.VMEM(send, jnp.float32), pltpu.VMEM(blocks.shape, blocks.dtype)]
    if len(given) == 1:
        body, where = whole_body, pltpu.HBM
        scratch += [pltpu.SemaphoreType.DMA((GROUPS,)), pltpu.VMEM((sources, configs, block_len), jnp.bfloat16)]
        scratch += [pltpu.SemaphoreType.DMA((GROUPS,))]
    else:
        body, where = pieces_body, pltpu.VMEM
        scratch += [pltpu.SemaphoreType.DMA((sources // span,))]
    given = [pltpu.with_memory_space_constraint(value, where) for value in given]
    blocks = pltpu.with_memory_space_constraint(blocks, pltpu.HBM)
    return pl.pallas_call(
        body,
        out_shape=[jax.ShapeDtypeStruct(piece, jnp.float32), jax.ShapeDtypeStruct(send, jnp.bfloat16)],
        grid_spec=pltpu.PrefetchScalarGridSpec(
            num_scalar_prefetch=3,
            grid=(1,),
            in_specs=[pl.BlockSpec(memory_space=where)] * len(given) + [pl.BlockSpec(memory_space=pltpu.HBM)],
            out_specs=[pl.BlockSpec(piece, lambda i, *_: (0, 0, 0)), pl.BlockSpec(send, lambda i, *_: (0, 0, 0))],
            scratch_shapes=scratch,
        ),
        compiler_params=pltpu.CompilerParams(vmem_limit_bytes=24 << 20),
        cost_estimate=pl.CostEstimate(
            flops=2 * n * configs * block_len * block_len,
            bytes_accessed=2 * (sources * configs * block_len + n * block_len * block_len),
            transcendentals=0,
        ),
        name="products",
    )(src, dst, place, *given, blocks)


def turn(value, axis, by):
    n = lax.axis_size(axis)
    return lax.ppermute(value, axis, [(i, (i + by) % n) for i in range(n)])


def after(values, *others):
    return lax.optimization_barrier((values, others))[0]


def spread_z(mine):
    return [mine] + [turn(mine, "zh", by) for by in TURNS[1:]]


def spread_x(column):
    return [column, turn(column, "x", 1), turn(column, "x", 3)]


def pass_on(near):
    half = near[0].shape[0] // 2
    near = near + [turn(near[1][:half], "x", 1), turn(near[2][half:], "x", 3)]
    return jnp.concatenate(near, axis=0)


def exchange_rows(send):
    return lax.all_to_all(send, ROW, 0, 0, tiled=True)


def add_rows(own, got):
    total = own
    for part in jnp.split(got, SHAPE[0] * SHAPE[1], axis=0):
        total = total + part.astype(jnp.float32)
    return total


def shards(x_init, gen_blocks, blk_src, blk_dst, reward, horizon):
    blocks = gen_blocks[0, 0]
    src = blk_src[0, 0]
    dst = blk_dst[0, 0]
    span = x_init.shape[0]
    half = x_init.shape[1] // 2
    weights = poisson_weights(horizon)
    reward_f = reward.astype(jnp.float32)[:, None, :]
    x, zh, core = (lax.axis_index(a) for a in COL)
    row = lax.axis_index("y") * SHAPE[1] + lax.axis_index("zl")
    place = [row]
    for other in range(2):
        for by_x in TURNS:
            for by_z in TURNS:
                place.append((((x - by_x) % 4) * 4 + (zh - by_z) % 4) * 2 + (core + other) % 2)
    place = jnp.stack(place).astype(jnp.int32)
    state_a, state_b = x_init[:, :half], x_init[:, half:]
    sum_a = weights[0] * reward_f * state_a
    sum_b = weights[0] * reward_f * state_b
    whole = lax.all_gather(state_a.astype(jnp.bfloat16), COL, axis=0, tiled=True)
    column = jnp.concatenate(spread_z(state_b.astype(jnp.bfloat16)), axis=0)
    near = spread_x(column)
    for iteration in range(STEPS):
        last = iteration + 1 == STEPS
        near = pass_on(near)
        own_b, send_b = products(src, dst, place, [near, turn(near, "core", 1)], blocks, span)
        own_a, send_a = products(src, dst, place, [after(whole, send_b)], blocks, span)
        got_b = after(exchange_rows(send_b), send_a)
        got_a = exchange_rows(after(send_a, got_b))
        state_b = state_b + add_rows(own_b, got_b)
        sum_b = sum_b + weights[iteration + 1] * reward_f * state_b
        state_a = state_a + add_rows(own_a, got_a)
        sum_a = sum_a + weights[iteration + 1] * reward_f * state_a
        if not last:
            low_a = state_a.astype(jnp.bfloat16)
            whole = lax.all_gather(low_a, COL, axis=0, tiled=True)
            low_b = after(state_b.astype(jnp.bfloat16), low_a)
            near = spread_x(jnp.concatenate(spread_z(low_b), axis=0))
    return (
        jnp.concatenate([state_a, state_b], axis=1),
        jnp.concatenate([sum_a, sum_b], axis=1),
    )


def solution(mesh):
    fine = Mesh(mesh.devices.reshape(SHAPE), AXES)
    rc = P((*ROW, *COL), None, None)
    in_specs = (
        rc,
        P(ROW, COL, None, None, None),
        P(ROW, COL, None),
        P(ROW, COL, None),
        P((*ROW, *COL), None),
        P(),
    )
    return jax.shard_map(shards, mesh=fine, in_specs=in_specs, out_specs=(rc, rc), check_vma=False)
```

```python
import jax
import jax.numpy as jnp
from jax import lax
from jax.experimental import pallas as pl
from jax.experimental.pallas import tpu as pltpu
from jax.sharding import Mesh, PartitionSpec as P

STEPS = 3
AXES = ("y", "zl", "x", "zh", "core")
SHAPE = (4, 2, 4, 4, 2)
ROW = ("y", "zl")
COL = ("x", "zh", "core")
GROUPS = 8
AHEAD = 3
TURNS = (0, 1, 3, 2)


def poisson_weights(horizon):
    rate_time = horizon[0]
    poisson_term = jnp.exp(-rate_time)
    cumulated = poisson_term
    weights = [(1.0 - cumulated) / rate_time]
    for iteration in range(STEPS):
        poisson_term = poisson_term * rate_time / (iteration + 1.0)
        cumulated = cumulated + poisson_term
        weights.append((1.0 - cumulated) / rate_time)
    return weights


def hand_out(place, own_ref, send_ref, acc):
    span = own_ref.shape[0]
    mine = pl.ds(place[0] * span, span)
    own_ref[...] = acc[mine]
    send_ref[...] = acc[...].astype(send_ref.dtype)
    send_ref[mine] = jnp.zeros(own_ref.shape, send_ref.dtype)


def whole_body(src, dst, place, given, blk, own_ref, send_ref, acc, held, sems, whole, more_sems):
    slots = held.shape[0] // GROUPS
    rows = whole.shape[0] // GROUPS

    def fetch(group):
        part = pl.ds(pl.multiple_of(group * rows, rows), rows)
        block = pl.ds(pl.multiple_of(group * slots, slots), slots)
        return (
            pltpu.make_async_copy(given.at[part], whole.at[part], more_sems.at[group]),
            pltpu.make_async_copy(blk.at[block], held.at[block], sems.at[group]),
        )

    for group in range(AHEAD):
        for copy in fetch(group):
            copy.start()
    acc[...] = jnp.zeros_like(acc)

    @pl.loop(0, GROUPS)
    def _(group):
        for copy in fetch(group):
            copy.wait()

        @pl.when(group + AHEAD < GROUPS)
        def _():
            for copy in fetch(group + AHEAD):
                copy.start()

        for slot in range(slots):
            at = group * slots + slot
            acc[dst[at]] += jnp.dot(whole[src[at]], held[at], preferred_element_type=jnp.float32)

    hand_out(place, own_ref, send_ref, acc)


def pieces_body(src, dst, place, *refs):
    pieces, (blk, own_ref, send_ref, acc, held, sems) = refs[:-6], refs[-6:]
    span = own_ref.shape[0]
    counts = [piece.shape[0] // span for piece in pieces]
    firsts = [sum(counts[:number]) for number in range(len(counts))]
    slots = held.shape[0] // sum(counts)

    def fetch(shard):
        there = pl.ds(pl.multiple_of(shard * slots, slots), slots)
        part = pl.ds(pl.multiple_of(place[1 + shard] * slots, slots), slots)
        return pltpu.make_async_copy(blk.at[part], held.at[there], sems.at[shard])

    ahead = 4 * AHEAD
    for shard in range(ahead):
        fetch(shard).start()
    acc[...] = jnp.zeros_like(acc)
    for first, count, piece in zip(firsts, counts, pieces):

        @pl.loop(0, count // 2)
        def _(pair):
            for one in range(2):
                at_z = pair * 2 + one
                fetch(first + at_z).wait()

                @pl.when(first + at_z + ahead < sum(counts))
                def _():
                    fetch(first + at_z + ahead).start()

                shard = place[1 + first + at_z]
                for slot in range(slots):
                    at = shard * slots + slot
                    row = src[at] + (at_z - shard) * span
                    block = held[(first + at_z) * slots + slot]
                    acc[dst[at]] += jnp.dot(piece[row], block, preferred_element_type=jnp.float32)

    hand_out(place, own_ref, send_ref, acc)


def products(src, dst, place, given, blocks, span):
    n, block_len, _ = blocks.shape
    configs = given[0].shape[1]
    targets = SHAPE[0] * SHAPE[1] * span
    sources = SHAPE[2] * SHAPE[3] * SHAPE[4] * span
    piece = (span, configs, block_len)
    send = (targets, configs, block_len)
    scratch = [pltpu.VMEM(send, jnp.float32), pltpu.VMEM(blocks.shape, blocks.dtype)]
    if len(given) == 1:
        body, where = whole_body, pltpu.HBM
        scratch += [pltpu.SemaphoreType.DMA((GROUPS,)), pltpu.VMEM((sources, configs, block_len), jnp.bfloat16)]
        scratch += [pltpu.SemaphoreType.DMA((GROUPS,))]
    else:
        body, where = pieces_body, pltpu.VMEM
        scratch += [pltpu.SemaphoreType.DMA((sources // span,))]
    given = [pltpu.with_memory_space_constraint(value, where) for value in given]
    blocks = pltpu.with_memory_space_constraint(blocks, pltpu.HBM)
    return pl.pallas_call(
        body,
        out_shape=[jax.ShapeDtypeStruct(piece, jnp.float32), jax.ShapeDtypeStruct(send, jnp.bfloat16)],
        grid_spec=pltpu.PrefetchScalarGridSpec(
            num_scalar_prefetch=3,
            grid=(1,),
            in_specs=[pl.BlockSpec(memory_space=where)] * len(given) + [pl.BlockSpec(memory_space=pltpu.HBM)],
            out_specs=[pl.BlockSpec(piece, lambda i, *_: (0, 0, 0)), pl.BlockSpec(send, lambda i, *_: (0, 0, 0))],
            scratch_shapes=scratch,
        ),
        compiler_params=pltpu.CompilerParams(vmem_limit_bytes=(20 if len(given) == 1 else 15) << 20),
        cost_estimate=pl.CostEstimate(
            flops=2 * n * configs * block_len * block_len,
            bytes_accessed=2 * (sources * configs * block_len + n * block_len * block_len),
            transcendentals=0,
        ),
        name="products",
    )(src, dst, place, *given, blocks)


def turn(value, axis, by):
    n = lax.axis_size(axis)
    return lax.ppermute(value, axis, [(i, (i + by) % n) for i in range(n)])


def after(values, *others):
    return lax.optimization_barrier((values, others))[0]


def spread_z(mine):
    return [mine] + [turn(mine, "zh", by) for by in TURNS[1:]]


def spread_x(column):
    return [column, turn(column, "x", 1), turn(column, "x", 3)]


def pass_on(near):
    half = near[0].shape[0] // 2
    later = [turn(near[1][:half], "x", 1), turn(near[2][half:], "x", 3)]
    return [jnp.concatenate(near, axis=0), jnp.concatenate(later, axis=0)]


def exchange_rows(send):
    return lax.all_to_all(send, ROW, 0, 0, tiled=True)


def add_rows(own, got):
    total = own
    for part in jnp.split(got, SHAPE[0] * SHAPE[1], axis=0):
        total = total + part.astype(jnp.float32)
    return total


def shards(x_init, gen_blocks, blk_src, blk_dst, reward, horizon):
    blocks = gen_blocks[0, 0]
    src = blk_src[0, 0]
    dst = blk_dst[0, 0]
    span = x_init.shape[0]
    half = x_init.shape[1] // 2
    weights = poisson_weights(horizon)
    reward_f = reward.astype(jnp.float32)[:, None, :]
    x, zh, core = (lax.axis_index(a) for a in COL)
    row = lax.axis_index("y") * SHAPE[1] + lax.axis_index("zl")
    place = [row]
    for other in range(2):
        for by_x in TURNS:
            for by_z in TURNS:
                place.append((((x - by_x) % 4) * 4 + (zh - by_z) % 4) * 2 + (core + other) % 2)
    place = jnp.stack(place).astype(jnp.int32)
    state_a, state_b = x_init[:, :half], x_init[:, half:]
    sum_a = weights[0] * reward_f * state_a
    sum_b = weights[0] * reward_f * state_b
    whole = lax.all_gather(state_a.astype(jnp.bfloat16), COL, axis=0, tiled=True)
    column = jnp.concatenate(spread_z(state_b.astype(jnp.bfloat16)), axis=0)
    near = spread_x(column)
    for iteration in range(STEPS):
        last = iteration + 1 == STEPS
        near = pass_on(near)
        far = [turn(piece, "core", 1) for piece in near]
        own_b, send_b = products(src, dst, place, near + far, blocks, span)
        own_a, send_a = products(src, dst, place, [after(whole, send_b)], blocks, span)
        got_b = after(exchange_rows(send_b), send_a)
        got_a = exchange_rows(after(send_a, got_b))
        state_b = state_b + add_rows(own_b, got_b)
        sum_b = sum_b + weights[iteration + 1] * reward_f * state_b
        state_a = state_a + add_rows(own_a, got_a)
        sum_a = sum_a + weights[iteration + 1] * reward_f * state_a
        if not last:
            low_a = state_a.astype(jnp.bfloat16)
            whole = lax.all_gather(low_a, COL, axis=0, tiled=True)
            low_b = after(state_b.astype(jnp.bfloat16), low_a)
            near = spread_x(jnp.concatenate(spread_z(low_b), axis=0))
    return (
        jnp.concatenate([state_a, state_b], axis=1),
        jnp.concatenate([sum_a, sum_b], axis=1),
    )


def solution(mesh):
    fine = Mesh(mesh.devices.reshape(SHAPE), AXES)
    rc = P((*ROW, *COL), None, None)
    in_specs = (
        rc,
        P(ROW, COL, None, None, None),
        P(ROW, COL, None),
        P(ROW, COL, None),
        P((*ROW, *COL), None),
        P(),
    )
    return jax.shard_map(shards, mesh=fine, in_specs=in_specs, out_specs=(rc, rc), check_vma=False)
```

```python
import jax
import jax.numpy as jnp
from jax import lax
from jax.experimental import pallas as pl
from jax.experimental.pallas import tpu as pltpu
from jax.sharding import Mesh, PartitionSpec as P

STEPS = 3
AXES = ("y", "zl", "x", "zh", "core")
SHAPE = (4, 2, 4, 4, 2)
ROW = ("y", "zl")
COL = ("x", "zh", "core")
GROUPS = 8
AHEAD = 3
TURNS = (0, 1, 3, 2)
Z_TURNS = (0, 2, 1, 3)


def poisson_weights(horizon):
    rate_time = horizon[0]
    poisson_term = jnp.exp(-rate_time)
    cumulated = poisson_term
    weights = [(1.0 - cumulated) / rate_time]
    for iteration in range(STEPS):
        poisson_term = poisson_term * rate_time / (iteration + 1.0)
        cumulated = cumulated + poisson_term
        weights.append((1.0 - cumulated) / rate_time)
    return weights


def hand_out(place, own_ref, send_ref, acc):
    span = own_ref.shape[0]
    mine = pl.ds(place[0] * span, span)
    own_ref[...] = acc[mine]
    send_ref[...] = acc[...].astype(send_ref.dtype)
    send_ref[mine] = jnp.zeros(own_ref.shape, send_ref.dtype)


def whole_body(src, dst, place, given, blk, own_ref, send_ref, acc, held, sems, whole, more_sems):
    slots = held.shape[0] // GROUPS
    rows = whole.shape[0] // GROUPS

    def fetch(group):
        part = pl.ds(pl.multiple_of(group * rows, rows), rows)
        block = pl.ds(pl.multiple_of(group * slots, slots), slots)
        return (
            pltpu.make_async_copy(given.at[part], whole.at[part], more_sems.at[group]),
            pltpu.make_async_copy(blk.at[block], held.at[block], sems.at[group]),
        )

    for group in range(AHEAD):
        for copy in fetch(group):
            copy.start()
    acc[...] = jnp.zeros_like(acc)

    @pl.loop(0, GROUPS)
    def _(group):
        for copy in fetch(group):
            copy.wait()

        @pl.when(group + AHEAD < GROUPS)
        def _():
            for copy in fetch(group + AHEAD):
                copy.start()

        for slot in range(slots):
            at = group * slots + slot
            acc[dst[at]] += jnp.dot(whole[src[at]], held[at], preferred_element_type=jnp.float32)

    hand_out(place, own_ref, send_ref, acc)


def pieces_body(src, dst, place, *refs):
    pieces, (blk, own_ref, send_ref, acc, held, sems) = refs[:-6], refs[-6:]
    span = own_ref.shape[0]
    counts = [piece.shape[0] // span for piece in pieces]
    firsts = [sum(counts[:number]) for number in range(len(counts))]
    slots = held.shape[0] // sum(counts)

    def fetch(shard):
        there = pl.ds(pl.multiple_of(shard * slots, slots), slots)
        part = pl.ds(pl.multiple_of(place[1 + shard] * slots, slots), slots)
        return pltpu.make_async_copy(blk.at[part], held.at[there], sems.at[shard])

    ahead = 4 * AHEAD
    for shard in range(ahead):
        fetch(shard).start()
    acc[...] = jnp.zeros_like(acc)
    for first, count, piece in zip(firsts, counts, pieces):

        @pl.loop(0, count // 2)
        def _(pair):
            for one in range(2):
                at_z = pair * 2 + one
                fetch(first + at_z).wait()

                @pl.when(first + at_z + ahead < sum(counts))
                def _():
                    fetch(first + at_z + ahead).start()

                shard = place[1 + first + at_z]
                for slot in range(slots):
                    at = shard * slots + slot
                    row = src[at] + (at_z - shard) * span
                    block = held[(first + at_z) * slots + slot]
                    acc[dst[at]] += jnp.dot(piece[row], block, preferred_element_type=jnp.float32)

    hand_out(place, own_ref, send_ref, acc)


def products(src, dst, place, given, blocks, span):
    n, block_len, _ = blocks.shape
    configs = given[0].shape[1]
    targets = SHAPE[0] * SHAPE[1] * span
    sources = SHAPE[2] * SHAPE[3] * SHAPE[4] * span
    piece = (span, configs, block_len)
    send = (targets, configs, block_len)
    scratch = [pltpu.VMEM(send, jnp.float32), pltpu.VMEM(blocks.shape, blocks.dtype)]
    if len(given) == 1:
        body, where = whole_body, pltpu.HBM
        scratch += [pltpu.SemaphoreType.DMA((GROUPS,)), pltpu.VMEM((sources, configs, block_len), jnp.bfloat16)]
        scratch += [pltpu.SemaphoreType.DMA((GROUPS,))]
    else:
        body, where = pieces_body, pltpu.VMEM
        scratch += [pltpu.SemaphoreType.DMA((sources // span,))]
    given = [pltpu.with_memory_space_constraint(value, where) for value in given]
    blocks = pltpu.with_memory_space_constraint(blocks, pltpu.HBM)
    return pl.pallas_call(
        body,
        out_shape=[jax.ShapeDtypeStruct(piece, jnp.float32), jax.ShapeDtypeStruct(send, jnp.bfloat16)],
        grid_spec=pltpu.PrefetchScalarGridSpec(
            num_scalar_prefetch=3,
            grid=(1,),
            in_specs=[pl.BlockSpec(memory_space=where)] * len(given) + [pl.BlockSpec(memory_space=pltpu.HBM)],
            out_specs=[pl.BlockSpec(piece, lambda i, *_: (0, 0, 0)), pl.BlockSpec(send, lambda i, *_: (0, 0, 0))],
            scratch_shapes=scratch,
        ),
        compiler_params=pltpu.CompilerParams(vmem_limit_bytes=24 << 20),
        cost_estimate=pl.CostEstimate(
            flops=2 * n * configs * block_len * block_len,
            bytes_accessed=2 * (sources * configs * block_len + n * block_len * block_len),
            transcendentals=0,
        ),
        name="products",
    )(src, dst, place, *given, blocks)


def turn(value, axis, by):
    n = lax.axis_size(axis)
    return lax.ppermute(value, axis, [(i, (i + by) % n) for i in range(n)])


def after(values, *others):
    return lax.optimization_barrier((values, others))[0]


def spread_z(mine):
    return [mine] + [turn(mine, "zh", by) for by in Z_TURNS[1:]]


def spread_x(column):
    return [column, turn(column, "x", 1), turn(column, "x", 3)]


def pass_on(near):
    half = near[0].shape[0] // 2
    near = near + [turn(near[1][:half], "x", 1), turn(near[2][half:], "x", 3)]
    return jnp.concatenate(near, axis=0)


def exchange_rows(send):
    return lax.all_to_all(send, ROW, 0, 0, tiled=True)


def add_rows(own, got):
    total = own
    for part in jnp.split(got, SHAPE[0] * SHAPE[1], axis=0):
        total = total + part.astype(jnp.float32)
    return total


def shards(x_init, gen_blocks, blk_src, blk_dst, reward, horizon):
    blocks = gen_blocks[0, 0]
    src = blk_src[0, 0]
    dst = blk_dst[0, 0]
    span = x_init.shape[0]
    half = x_init.shape[1] * 40 // 64
    weights = poisson_weights(horizon)
    reward_f = reward.astype(jnp.float32)[:, None, :]
    x, zh, core = (lax.axis_index(a) for a in COL)
    row = lax.axis_index("y") * SHAPE[1] + lax.axis_index("zl")
    place = [row]
    for other in range(2):
        for by_x in TURNS:
            for by_z in Z_TURNS:
                place.append((((x - by_x) % 4) * 4 + (zh - by_z) % 4) * 2 + (core + other) % 2)
    place = jnp.stack(place).astype(jnp.int32)
    state_a, state_b = x_init[:, :half], x_init[:, half:]
    sum_a = weights[0] * reward_f * state_a
    sum_b = weights[0] * reward_f * state_b
    whole = lax.all_gather(state_a.astype(jnp.bfloat16), COL, axis=0, tiled=True)
    column = jnp.concatenate(spread_z(state_b.astype(jnp.bfloat16)), axis=0)
    near = spread_x(column)
    for iteration in range(STEPS):
        last = iteration + 1 == STEPS
        near = pass_on(near)
        own_b, send_b = products(src, dst, place, [near, turn(near, "core", 1)], blocks, span)
        own_a, send_a = products(src, dst, place, [after(whole, send_b)], blocks, span)
        got_b = after(exchange_rows(send_b), send_a)
        got_a = exchange_rows(after(send_a, got_b))
        state_b = state_b + add_rows(own_b, got_b)
        sum_b = sum_b + weights[iteration + 1] * reward_f * state_b
        state_a = state_a + add_rows(own_a, got_a)
        sum_a = sum_a + weights[iteration + 1] * reward_f * state_a
        if not last:
            low_a = state_a.astype(jnp.bfloat16)
            whole = lax.all_gather(low_a, COL, axis=0, tiled=True)
            low_b = after(state_b.astype(jnp.bfloat16), low_a)
            near = spread_x(jnp.concatenate(spread_z(low_b), axis=0))
    return (
        jnp.concatenate([state_a, state_b], axis=1),
        jnp.concatenate([sum_a, sum_b], axis=1),
    )


def solution(mesh):
    fine = Mesh(mesh.devices.reshape(SHAPE), AXES)
    rc = P((*ROW, *COL), None, None)
    in_specs = (
        rc,
        P(ROW, COL, None, None, None),
        P(ROW, COL, None),
        P(ROW, COL, None),
        P((*ROW, *COL), None),
        P(),
    )
    return jax.shard_map(shards, mesh=fine, in_specs=in_specs, out_specs=(rc, rc), check_vma=False)
```
